32 devices in a mesh: probe: 4 (over z), gx: 4 (over x, core), gy: 2 (over y).
Axes of the slice: x: 2, y: 2, z: 4, core: 2. Of those that a mesh axis runs over, the one named last changes fastest.
Arguments:
- wave_prev: float32 [4, 128, 256, 256], P('probe', 'gx', 'gy'), may hold values from -6 to 6
- wave_cur: float32 [4, 128, 256, 256], P('probe', 'gx', 'gy'), may hold values from -6 to 6
- courant: float32 [128, 256, 256], P('gx', 'gy'), may hold values from 0.02 to 0.16
- perturb: float32 [4, 128, 256, 256], P('probe', 'gx', 'gy'), may hold values from -4 to 4
- snapshots: bfloat16 [8, 128, 256, 256], P('probe', 'gx', 'gy'), may hold values from -6 to 6
- step_slots: int32 [6], replicated, may hold values from 0 to 7, as said below
- precond: float32 [256], replicated, may hold values from 0.5 to 2
- probe_ids: int32 [4], P('probe'), may hold values from 0 to 255, as said below
Outputs:
- earlier: float32 [4, 128, 256, 256], P('probe', 'gx', 'gy')
- latest: float32 [4, 128, 256, 256], P('probe', 'gx', 'gy')
The draws below stay inside these ranges and needn't reach their ends.
Inputs may be any that keep to these rules, and one draw needn't show every extreme that they name: `step_slots`: distinct slots; 0 and 7 are always among them. `probe_ids`: distinct indices; 0 and 255 are always among them.
All inputs are finite; a program needn't handle non-finite values.
Results may differ from the reference program's by a relative error of at most 0.0003.
Values may be sent and summed in bfloat16 or wider, within the bound.
A program may use at most 192 MiB of HBM per device.

```python
import math
import jax
import jax.numpy as jnp

CZ = 256
STEPS = 4
NPROBE_ALL = 256
PROBES = 4
SLOTS = 8
NSNAP = 6
NX = 128
NY = 256


def pick_distinct(key, count, total):
    inner = jax.random.permutation(key, total - 2)[:count - 2].astype(jnp.int32) + 1
    values = jnp.concatenate([jnp.array([0, total - 1], jnp.int32), inner])
    return jax.random.permutation(jax.random.fold_in(key, 7), values).astype(jnp.int32)


def draw_step_slots(key, part):
    return pick_distinct(jax.random.fold_in(key, 11), NSNAP, SLOTS)


def draw_probe_ids(key, part):
    return pick_distinct(jax.random.fold_in(key, 13), PROBES, NPROBE_ALL)


def steps_of(stream_key, shape, pieces, low, high):
    def one(position, parts):
        draws = jax.random.uniform(jax.random.fold_in(jax.random.fold_in(stream_key, 6), position), (parts,), jnp.float32, low / len(pieces), high / len(pieces))
        return jnp.repeat(jnp.exp(draws), shape[position] // parts).reshape((-1,) + (1,) * (len(shape) - position - 1))

    gain = one(*pieces[0])
    for cut in pieces[1:]:
        gain = gain * one(*cut)
    return gain


def normal_values(rng, extent, spread, limit, cuts=(), kind=jnp.bfloat16):
    result = jax.random.normal(rng, extent, jnp.float32) * spread
    if len(cuts) > 0:
        result = steps_of(rng, extent, cuts, -0.22, 0.18) * result
    return jnp.clip(result, min=-limit, max=limit).astype(kind)


def setup_inputs(seed: int = 0) -> dict:
    key_list = jax.random.split(jax.random.key(seed), 9)
    return {
        "wave_prev": normal_values(key_list[0], (PROBES, NX, NY, CZ), 1.0, 6.0, ((0, 4), (1, 4), (2, 2)), jnp.float32),
        "wave_cur": normal_values(key_list[1], (PROBES, NX, NY, CZ), 1.0, 6.0, ((0, 4), (1, 4), (2, 2)), jnp.float32),
        "courant": jnp.clip(jnp.exp(math.log(0.16) - 2.0794415 * jax.random.uniform(key_list[2], (NX, NY, CZ), jnp.float32) ** steps_of(key_list[2], (NX, NY, CZ), ((0, 4), (1, 2)), -0.2, 0.2)), 0.02, 0.16),
        "perturb": normal_values(key_list[3], (PROBES, NX, NY, CZ), 0.5, 4.0, ((0, 4), (1, 4), (2, 2)), jnp.float32),
        "snapshots": normal_values(key_list[4], (SLOTS, NX, NY, CZ), 1.0, 6.0, ((0, 4), (1, 4), (2, 2))),
        "step_slots": draw_step_slots(jax.random.fold_in(key_list[8], 71), 0),
        "precond": jnp.clip(jnp.exp(jax.random.uniform(key_list[6], (NPROBE_ALL,), jnp.float32, math.log(0.5), math.log(2.0))), 0.5, 2.0),
        "probe_ids": draw_probe_ids(jax.random.fold_in(key_list[8], 71), 0),
    }


COEFFS = (-205.0 / 72.0, 8.0 / 5.0, -1.0 / 5.0, 8.0 / 315.0, -1.0 / 560.0)


def stencil(padded, field):
    extent_x = field.shape[1]
    extent_y = field.shape[2]
    extent_z = field.shape[3]
    total = (3.0 * COEFFS[0]) * field
    for offset in range(1, 5):
        factor = COEFFS[offset]
        along = padded[:, 4 + offset:4 + offset + extent_x, 4:4 + extent_y, 4:4 + extent_z]
        along = along + padded[:, 4 - offset:4 - offset + extent_x, 4:4 + extent_y, 4:4 + extent_z]
        along = along + padded[:, 4:4 + extent_x, 4 + offset:4 + offset + extent_y, 4:4 + extent_z]
        along = along + padded[:, 4:4 + extent_x, 4 - offset:4 - offset + extent_y, 4:4 + extent_z]
        along = along + padded[:, 4:4 + extent_x, 4:4 + extent_y, 4 + offset:4 + offset + extent_z]
        along = along + padded[:, 4:4 + extent_x, 4:4 + extent_y, 4 - offset:4 - offset + extent_z]
        total = total + factor * along
    return total


def reference(wave_prev, wave_cur, courant, perturb, snapshots, step_slots, precond, probe_ids):
    weight = jnp.take(precond, probe_ids.astype(jnp.int32), axis=0)
    scaled = weight[:, None, None, None] * perturb
    frames = jnp.take(snapshots, step_slots.astype(jnp.int32), axis=0).astype(jnp.float32)
    previous = wave_prev
    current = wave_cur
    for index in range(STEPS):
        source = frames[index + 2] - 2.0 * frames[index + 1] + frames[index]
        padded = jnp.pad(current, ((0, 0), (4, 4), (4, 4), (4, 4)))
        laplace = stencil(padded, current)
        following = 2.0 * current - previous + courant[None] * laplace - scaled * source[None]
        previous = current
        current = following
    return previous, current
```

```python
import functools

import jax
import jax.numpy as jnp
import ml_dtypes
import numpy as np
from jax import lax
from jax.experimental import pallas as pl
from jax.experimental.pallas import tpu as pltpu
from jax.sharding import PartitionSpec as P

STEPS = 4
COEFFS = (-205.0 / 72.0, 8.0 / 5.0, -1.0 / 5.0, 8.0 / 315.0, -1.0 / 560.0)
W = 4
PAD = 16
AHEAD = 2
RING = 8
MESH = pl.DeviceIdType.MESH


def band(rows, cols, shift):
    out = np.zeros((rows, cols), np.float64)
    for r in range(rows):
        for k in range(1, 5):
            for c in (r + shift - k, r + shift + k):
                if 0 <= c < cols:
                    out[r, c] += COEFFS[k]
    return out


def halves(matrix):
    high = matrix.astype(ml_dtypes.bfloat16)
    low = (matrix - high.astype(np.float64)).astype(ml_dtypes.bfloat16)
    return high, low


def kernel(
    n_probe,
    n_gx,
    n_gy,
    skips,
    slots,
    precond,
    ids,
    ymat,
    zmat,
    prev_hbm,
    cur_hbm,
    cou_hbm,
    per_hbm,
    snap_hbm,
    early_hbm,
    late_hbm,
    field,
    cou,
    per,
    own,
    first,
    up,
    down,
    frames,
    load_sem,
    out_sem,
    up_send,
    up_recv,
    down_send,
    down_recv,
    first_up_send,
    first_up_recv,
    first_down_send,
    first_down_recv,
    wide_send,
    wide_recv,
    x_send,
    x_recv,
    y_send,
    y_recv,
):
    z = lax.axis_index("probe")
    gx = lax.axis_index("gx")
    gy = lax.axis_index("gy")
    nx, ny, nz = cou.shape
    slot_dev = own.shape[0]
    n_snap = slots.shape[0]
    n_msg = n_snap - skips
    run = nx - AHEAD
    total = n_msg * run
    lag = slot_dev * AHEAD
    body_x = pl.ds(W, nx)
    body_y = pl.ds(PAD, ny)

    def loop(low, high, fn):
        def step(i, carry):
            fn(i)
            return carry

        lax.fori_loop(low, high, step, 0)

    def spot(q):
        half = lax.div(q, 2)
        return jnp.where(lax.rem(q, 2) == 0, half, nx - 1 - half)

    loads = [
        pltpu.make_async_copy(snap_hbm, own, load_sem.at[0]),
        pltpu.make_async_copy(cur_hbm.at[0], field.at[0, body_x, body_y], load_sem.at[1]),
        pltpu.make_async_copy(prev_hbm.at[0], field.at[1, body_x, body_y], load_sem.at[2]),
        pltpu.make_async_copy(cou_hbm, cou, load_sem.at[3]),
        pltpu.make_async_copy(per_hbm.at[0], per, load_sem.at[4]),
    ]
    loads[0].start()

    zero_plane = jnp.zeros((ny, nz), jnp.float32)
    zero_rows = jnp.zeros((PAD, nz), jnp.float32)
    for b in range(2):
        for x in range(W):
            field[b, x, body_y] = zero_plane
            field[b, W + nx + x, body_y] = zero_plane

        def clear(x, b=b):
            field[b, W + x, pl.ds(0, PAD)] = zero_rows
            field[b, W + x, pl.ds(PAD + ny, PAD)] = zero_rows

        loop(0, nx, clear)

    sides = (
        (z < n_probe - 1, {"probe": z + 1}),
        (z > 0, {"probe": z - 1}),
        (gx < n_gx - 1, {"gx": gx + 1}),
        (gx > 0, {"gx": gx - 1}),
        (gy < n_gy - 1, {"gy": gy + 1}),
        (gy > 0, {"gy": gy - 1}),
    )
    barrier = pltpu.get_barrier_semaphore()
    for there, target in sides:

        @pl.when(there)
        def _():
            pl.semaphore_signal(barrier, inc=1, device_id=target, device_id_type=MESH)

    loads[0].wait()
    for w in range(slot_dev):
        for q in range(AHEAD):
            first[z * slot_dev + w, q] = own[w, q // 2 if q % 2 == 0 else nx - 1 - q // 2]
    pl.semaphore_wait(barrier, sum(there.astype(jnp.int32) for there, _ in sides))

    halo_out = (
        (pl.ds(nx, W), body_y, pl.ds(0, W), body_y),
        (pl.ds(W, W), body_y, pl.ds(W + nx, W), body_y),
        (body_x, pl.ds(PAD + ny - 8, 8), body_x, pl.ds(PAD - 8, 8)),
        (body_x, pl.ds(PAD, 8), body_x, pl.ds(PAD + ny, 8)),
    )
    back = (1, 0, 3, 2)

    def wide_halo(side):
        sx, sy, dx, dy = halo_out[side]
        return pltpu.make_async_remote_copy(
            src_ref=field.at[0, sx, sy],
            dst_ref=field.at[0, dx, dy],
            send_sem=wide_send.at[side],
            recv_sem=wide_recv.at[side],
            device_id=sides[2 + side][1],
            device_id_type=MESH,
        )

    def x_halo(e, side, i):
        from_x = W + nx - 1 - i if side == 0 else W + i
        to_x = W - 1 - i if side == 0 else W + nx + i
        return pltpu.make_async_remote_copy(
            src_ref=field.at[e % 2, from_x, body_y],
            dst_ref=field.at[e % 2, to_x, body_y],
            send_sem=x_send.at[e - 1, side, i],
            recv_sem=x_recv.at[e - 1, side, i],
            device_id=sides[2 + side][1],
            device_id_type=MESH,
        )

    def y_halo(e, side, q):
        _, sy, _, dy = halo_out[2 + side]
        x = W + spot(q)
        return pltpu.make_async_remote_copy(
            src_ref=field.at[e % 2, x, sy],
            dst_ref=field.at[e % 2, x, dy],
            send_sem=y_send.at[e - 1, side, q],
            recv_sem=y_recv.at[e - 1, side, q],
            device_id=sides[4 + side][1],
            device_id_type=MESH,
        )

    def each_halo(e, q, act):
        for side in range(2):
            edge = (lax.rem(q, 2) == 1 - side) & (q < 2 * W)

            @pl.when(sides[2 + side][0] & edge)
            def _():
                act(x_halo(e, side, lax.div(q, 2)))

        for side in range(2):

            @pl.when(sides[4 + side][0])
            def _():
                act(y_halo(e, side, q))

    def halo_start(e, q):
        each_halo(e, q, lambda copy: copy.start())

    def halo_sent(e, q):
        each_halo(e, q, lambda copy: copy.wait_send())

    def halo_wait(e, q):
        for side in range(2):

            @pl.when(sides[2 + side][0] & (q == 0))
            def _():
                for i in range(W):
                    x_halo(e, back[side], i).wait_recv()

        for side in range(2):

            @pl.when(sides[4 + side][0])
            def _():
                y_halo(e, 1 - side, q).wait_recv()

    owner = [lax.div(slots[j], slot_dev) for j in range(n_snap)]

    def skipped(end, slot):
        if skips == 1:
            at = jnp.int32(0)
            for j in range(n_snap):
                at = jnp.where(slots[j] == slot, j, at)
            return (at,)
        low = jnp.int32(n_snap)
        high = jnp.int32(-1)
        for j in range(n_snap):
            low = jnp.where(owner[j] == end, jnp.minimum(low, j), low)
            high = jnp.where(owner[j] == end, j, high)
        return (low, high)

    not_up = skipped(n_probe - 1, n_probe * slot_dev - 1)
    not_down = skipped(0, 0)

    up_way = (up, first_up_send, first_up_recv, up_send, up_recv, {"probe": z + 1}, z < n_probe - 1)
    down_way = (down, first_down_send, first_down_recv, down_send, down_recv, {"probe": z - 1}, z > 0)

    def head_link(way, slot, q):
        return pltpu.make_async_remote_copy(
            src_ref=first.at[slot, q],
            dst_ref=first.at[slot, q],
            send_sem=way[1].at[slot, q],
            recv_sem=way[2].at[slot, q],
            device_id=way[5],
            device_id_type=MESH,
        )

    def link(way, k):
        return pltpu.make_async_remote_copy(
            src_ref=way[0].at[k],
            dst_ref=way[0].at[k],
            send_sem=way[3].at[k],
            recv_sem=way[4].at[k],
            device_id=way[5],
            device_id_type=MESH,
        )

    def relay(s, way, hops, step, missing):
        buf, forwards = way[0], way[6]

        @pl.when(s < lag * hops)
        def _():
            group = lax.div(s, lag)
            item = s - group * lag
            w = lax.div(item, AHEAD)
            copy = head_link(way, (z - step * (group + 1)) * slot_dev + w, item - w * AHEAD)
            copy.wait_recv()

            @pl.when(forwards)
            def _():
                copy.start()

        k = s - lag * hops

        @pl.when((k >= 0) & (k < total))
        def _():
            m = lax.div(k, run)
            x = spot(AHEAD + k - m * run)
            position = m
            for place in missing:
                position = position + jnp.where(position >= place, 1, 0)
            slot = slots[position]
            mine = lax.div(slot, slot_dev) == z
            which = lax.rem(slot, slot_dev)

            @pl.when(hops == 0)
            def _():
                buf[k] = own[which, x]

            @pl.when(hops > 0)
            def _():
                link(way, k).wait_recv()
                buf[k] = lax.select(mine, own[which, x], buf[k])

            @pl.when(forwards)
            def _():
                link(way, k).start()

            @pl.when(forwards & (k >= RING))
            def _():
                link(way, k - RING).wait_send()

    def comm(s):
        relay(s, up_way, z, 1, not_up)
        relay(s, down_way, n_probe - 1 - z, -1, not_down)

    def fetch(j, q):
        @pl.when(q < AHEAD)
        def _():
            frames[j % 3, q] = first[slots[j], q]

        @pl.when(q >= AHEAD)
        def _():
            def pick(buf, missing):
                count = sum(jnp.where(place < j, 1, 0) for place in missing)
                found = None
                for d in range(skips + 1):
                    if 0 <= j - d < n_msg:
                        value = buf[(j - d) * run + q - AHEAD]
                        found = value if found is None else lax.select(count == d, value, found)
                return found

            from_up = owner[j] <= z
            for place in not_up:
                from_up = from_up & (place != j)
            frames[j % 3, q] = lax.select(from_up, pick(up, not_up), pick(down, not_down))

    weight = precond[ids[0]]

    def out(last, x):
        return pltpu.make_async_copy(
            field.at[1 - last, W + x, body_y],
            (late_hbm if last else early_hbm).at[0, x],
            out_sem.at[last, x],
        )

    def plane(n, q):
        a, b = n % 2, 1 - n % 2
        x = spot(q)
        if n > 0:
            halo_wait(n, q)
        if n > 1:
            halo_sent(n - 1, q)
        if n == 0:
            fetch(0, q)
            fetch(1, q)
        fetch(n + 2, q)
        source = (
            frames[(n + 2) % 3, q].astype(jnp.float32)
            - 2.0 * frames[(n + 1) % 3, q].astype(jnp.float32)
            + frames[n % 3, q].astype(jnp.float32)
        )
        padded = field[a, x + W]
        high = padded.astype(jnp.bfloat16)
        low = (padded - high.astype(jnp.float32)).astype(jnp.bfloat16)
        lap = jnp.dot(
            ymat[...],
            jnp.concatenate([high, low, high], axis=0),
            preferred_element_type=jnp.float32,
        )
        high = high[PAD : PAD + ny]
        low = low[PAD : PAD + ny]
        lap = lap + jnp.dot(
            jnp.concatenate([high, low, high], axis=1),
            zmat[...],
            preferred_element_type=jnp.float32,
        )
        here = field[a, x + W, body_y]
        lap = lap + (3.0 * COEFFS[0]) * here
        for k in range(1, 5):
            lap = lap + COEFFS[k] * (field[a, x + W + k, body_y] + field[a, x + W - k, body_y])
        field[b, x + W, body_y] = (
            2.0 * here - field[b, x + W, body_y] + cou[x] * lap - (weight * per[x]) * source
        )
        if n < STEPS - 1:
            halo_start(n + 1, q)
        if n == STEPS - 2:
            out(0, x).start()
        if n == STEPS - 1:
            out(1, x).start()

    for w in range(slot_dev):
        for q in range(AHEAD):
            for way in (up_way, down_way):

                @pl.when(way[6])
                def _():
                    head_link(way, z * slot_dev + w, q).start()

    for load in loads[1:]:
        load.start()
    lead = lag * (n_probe - 1)
    loop(0, lead, comm)
    loads[1].wait()
    for side in range(4):

        @pl.when(sides[2 + side][0])
        def _():
            wide_halo(side).start()

    loop(lead, lead + 2 * run, comm)
    for load in loads[2:]:
        load.wait()
    for side in range(4):

        @pl.when(sides[2 + side][0])
        def _():
            wide_halo(side).wait_send()
            wide_halo(back[side]).wait_recv()

    for slot in range(n_probe * slot_dev):
        for q in range(AHEAD):

            @pl.when(up_way[6] & (slot < (z + 1) * slot_dev))
            def _():
                head_link(up_way, slot, q).wait_send()

            @pl.when(down_way[6] & (slot >= z * slot_dev))
            def _():
                head_link(down_way, slot, q).wait_send()

    def comms(m, q):
        @pl.when((q >= AHEAD) & (q < nx))
        def _():
            comm(lead + m * run + q - AHEAD)

    for m in range(2, n_msg - 1):

        def simple(q, m=m):
            comms(m, q)
            plane(m - 2, q)

        loop(0, nx, simple)

    base = n_msg - 3
    levels = STEPS - base

    def done(level, q):
        if level == 0:
            return jnp.minimum(q, nx)
        w = 2 * W
        steady = q - w * level
        start = 2 * (q - w * level - w // 2)
        return jnp.clip(jnp.minimum(steady, start), 0, nx)

    def front(q):
        comms(n_msg - 1, q)
        for level in range(levels):
            loop(done(level, q), done(level, q + 1), functools.partial(plane, base + level))

    loop(0, nx + 2 * W * (levels - 1), front)

    def finish(k):
        for way in (up_way, down_way):

            @pl.when(way[6])
            def _():
                link(way, k).wait_send()

    loop(total - RING, total, finish)

    def flush(x):
        halo_sent(STEPS - 1, x)
        out(0, x).wait()
        out(1, x).wait()

    loop(0, nx, flush)


def steps(
    sizes, skips, wave_prev, wave_cur, courant, perturb, snapshots, step_slots, precond, probe_ids
):
    nx, ny, nz = courant.shape
    slot_dev = snapshots.shape[0]
    total = (step_slots.shape[0] - skips) * (nx - AHEAD)
    y_high, y_low = halves(band(ny, ny + 2 * PAD, PAD))
    z_high, z_low = halves(band(nz, nz, 0))
    ymat = jnp.asarray(np.concatenate([y_high, y_high, y_low], axis=1))
    zmat = jnp.asarray(np.concatenate([z_high, z_high, z_low], axis=0))
    smem = pl.BlockSpec(memory_space=pltpu.SMEM)
    vmem = pl.BlockSpec(memory_space=pltpu.VMEM)
    hbm = pl.BlockSpec(memory_space=pl.ANY)
    wave = jax.ShapeDtypeStruct(wave_cur.shape, jnp.float32)
    dma = pltpu.SemaphoreType.DMA
    messages = pltpu.VMEM((total, ny, nz), jnp.bfloat16)
    return pl.pallas_call(
        functools.partial(kernel, *sizes, skips),
        out_shape=(wave, wave),
        in_specs=[smem, smem, smem, vmem, vmem] + [hbm] * 5,
        out_specs=(hbm, hbm),
        scratch_shapes=[
            pltpu.VMEM((2, nx + 2 * W, ny + 2 * PAD, nz), jnp.float32),
            pltpu.VMEM((nx, ny, nz), jnp.float32),
            pltpu.VMEM((nx, ny, nz), jnp.float32),
            pltpu.VMEM((slot_dev, nx, ny, nz), jnp.bfloat16),
            pltpu.VMEM((sizes[0] * slot_dev, AHEAD, ny, nz), jnp.bfloat16),
            messages,
            messages,
            pltpu.VMEM((3, nx, ny, nz), jnp.bfloat16),
            dma((5,)),
            dma((2, nx)),
            dma((total,)),
            dma((total,)),
            dma((total,)),
            dma((total,)),
            dma((sizes[0] * slot_dev, AHEAD)),
            dma((sizes[0] * slot_dev, AHEAD)),
            dma((sizes[0] * slot_dev, AHEAD)),
            dma((sizes[0] * slot_dev, AHEAD)),
            dma((4,)),
            dma((4,)),
            dma((STEPS - 1, 2, W)),
            dma((STEPS - 1, 2, W)),
            dma((STEPS - 1, 2, nx)),
            dma((STEPS - 1, 2, nx)),
        ],
        compiler_params=pltpu.CompilerParams(
            collective_id=skips - 1, has_side_effects=True, vmem_limit_bytes=60 * 1024 * 1024
        ),
    )(
        step_slots,
        precond,
        probe_ids,
        ymat,
        zmat,
        wave_prev,
        wave_cur,
        courant,
        perturb,
        snapshots,
    )


def shards(sizes, *args):
    snapshots, step_slots = args[4], args[5]
    n_probe, slot_dev = sizes[0], snapshots.shape[0]
    if slot_dev == 2:
        owner = step_slots // slot_dev
        ends = (jnp.sum(owner == 0) == slot_dev) & (jnp.sum(owner == n_probe - 1) == slot_dev)
        return lax.cond(
            ends,
            functools.partial(steps, sizes, 2),
            functools.partial(steps, sizes, 1),
            *args,
        )
    return steps(sizes, 1, *args)


def solution(mesh):
    placed = (
        P("probe", "gx", "gy", None),
        P("probe", "gx", "gy", None),
        P("gx", "gy", None),
        P("probe", "gx", "gy", None),
        P("probe", "gx", "gy", None),
        P(),
        P(),
        P("probe"),
    )
    sizes = (mesh.shape["probe"], mesh.shape["gx"], mesh.shape["gy"])
    return jax.shard_map(
        functools.partial(shards, sizes),
        mesh=mesh,
        in_specs=placed,
        out_specs=(P("probe", "gx", "gy", None), P("probe", "gx", "gy", None)),
        check_vma=False,
    )
```

```python
import functools

import jax
import jax.numpy as jnp
import ml_dtypes
import numpy as np
from jax import lax
from jax.experimental import pallas as pl
from jax.experimental.pallas import tpu as pltpu
from jax.sharding import PartitionSpec as P

STEPS = 4
COEFFS = (-205.0 / 72.0, 8.0 / 5.0, -1.0 / 5.0, 8.0 / 315.0, -1.0 / 560.0)
W = 4
PAD = 16
AHEAD = 2
PARTS = 4
MESH = pl.DeviceIdType.MESH


def band(rows, cols, shift):
    out = np.zeros((rows, cols), np.float64)
    for r in range(rows):
        for k in range(1, 5):
            for c in (r + shift - k, r + shift + k):
                if 0 <= c < cols:
                    out[r, c] += COEFFS[k]
    return out


def halves(matrix):
    high = matrix.astype(ml_dtypes.bfloat16)
    low = (matrix - high.astype(np.float64)).astype(ml_dtypes.bfloat16)
    return high, low


def kernel(
    n_probe,
    n_gx,
    n_gy,
    skips,
    slots,
    precond,
    ids,
    ymat,
    zmat,
    prev_hbm,
    cur_hbm,
    cou_hbm,
    per_hbm,
    snap_hbm,
    early,
    late,
    field,
    cou,
    per,
    own,
    first,
    up,
    down,
    frames,
    load_sem,
    up_send,
    up_recv,
    down_send,
    down_recv,
    wide_send,
    wide_recv,
    x_send,
    x_recv,
    y_send,
    y_recv,
):
    z = lax.axis_index("probe")
    gx = lax.axis_index("gx")
    gy = lax.axis_index("gy")
    nx, ny, nz = cou.shape
    slot_dev = own.shape[0]
    n_snap = slots.shape[0]
    n_msg = n_snap - skips
    run = nx - AHEAD
    total = n_msg * run
    lag = slot_dev * AHEAD
    ring = up_send.shape[0]
    body_x = pl.ds(W, nx)
    body_y = pl.ds(PAD, ny)

    def loop(low, high, fn):
        def step(i, carry):
            fn(i)
            return carry

        lax.fori_loop(low, high, step, 0)

    def spot(q):
        half = lax.div(q, 2)
        return jnp.where(lax.rem(q, 2) == 0, half, nx - 1 - half)

    loads = [
        pltpu.make_async_copy(snap_hbm, own, load_sem.at[0]),
        pltpu.make_async_copy(cur_hbm.at[0], field.at[0, body_x, body_y], load_sem.at[1]),
        pltpu.make_async_copy(prev_hbm.at[0], field.at[1, body_x, body_y], load_sem.at[2]),
        pltpu.make_async_copy(cou_hbm, cou, load_sem.at[3]),
        pltpu.make_async_copy(per_hbm.at[0], per, load_sem.at[4]),
    ]
    loads[0].start()

    zero_plane = jnp.zeros((ny, nz), jnp.float32)
    zero_rows = jnp.zeros((PAD, nz), jnp.float32)
    for b in range(2):
        for x in range(W):
            field[b, x, body_y] = zero_plane
            field[b, W + nx + x, body_y] = zero_plane

        def clear(x, b=b):
            field[b, W + x, pl.ds(0, PAD)] = zero_rows
            field[b, W + x, pl.ds(PAD + ny, PAD)] = zero_rows

        loop(0, nx, clear)

    sides = (
        (z < n_probe - 1, {"probe": z + 1}),
        (z > 0, {"probe": z - 1}),
        (gx < n_gx - 1, {"gx": gx + 1}),
        (gx > 0, {"gx": gx - 1}),
    )
    across = {"gy": 1 - gy}
    barrier = pltpu.get_barrier_semaphore()
    for there, target in sides:

        @pl.when(there)
        def _():
            pl.semaphore_signal(barrier, inc=1, device_id=target, device_id_type=MESH)

    pl.semaphore_signal(barrier, inc=1, device_id=across, device_id_type=MESH)
    loads[0].wait()
    for w in range(slot_dev):
        for q in range(AHEAD):
            first[z * slot_dev + w, q] = own[w, q // 2 if q % 2 == 0 else nx - 1 - q // 2]
    pl.semaphore_wait(barrier, 1 + sum(there.astype(jnp.int32) for there, _ in sides))

    y_from = pl.ds(pl.multiple_of(jnp.where(gy == 0, PAD + ny - 8, PAD), 8), 8)
    y_to = pl.ds(pl.multiple_of(jnp.where(gy == 0, PAD - 8, PAD + ny), 8), 8)

    def wide_halo(side):
        from_x, from_y, to_x, to_y = (
            (pl.ds(nx, W), body_y, pl.ds(0, W), body_y),
            (pl.ds(W, W), body_y, pl.ds(W + nx, W), body_y),
            (body_x, y_from, body_x, y_to),
        )[side]
        return pltpu.make_async_remote_copy(
            src_ref=field.at[0, from_x, from_y],
            dst_ref=field.at[0, to_x, to_y],
            send_sem=wide_send.at[side],
            recv_sem=wide_recv.at[side],
            device_id=across if side == 2 else sides[2 + side][1],
            device_id_type=MESH,
        )

    def x_halo(e, side, i):
        from_x = W + nx - 1 - i if side == 0 else W + i
        to_x = W - 1 - i if side == 0 else W + nx + i
        return pltpu.make_async_remote_copy(
            src_ref=field.at[e % 2, from_x, body_y],
            dst_ref=field.at[e % 2, to_x, body_y],
            send_sem=x_send.at[side, i],
            recv_sem=x_recv.at[e % 2, side, i],
            device_id=sides[2 + side][1],
            device_id_type=MESH,
        )

    def y_halo(e, q):
        x = W + spot(q)
        return pltpu.make_async_remote_copy(
            src_ref=field.at[e % 2, x, y_from],
            dst_ref=field.at[e % 2, x, y_to],
            send_sem=y_send.at[q],
            recv_sem=y_recv.at[e % 2, q],
            device_id=across,
            device_id_type=MESH,
        )

    def each_halo(e, q, act):
        for side in range(2):
            edge = (lax.rem(q, 2) == 1 - side) & (q < 2 * W)

            @pl.when(sides[2 + side][0] & edge)
            def _():
                act(x_halo(e, side, lax.div(q, 2)))

        act(y_halo(e, q))

    def halo_start(e, q):
        each_halo(e, q, lambda copy: copy.start())

    def halo_sent(e, q):
        each_halo(e, q, lambda copy: copy.wait_send())

    def halo_wait(e, q):
        for side in range(2):

            @pl.when(sides[2 + side][0] & (q == 0))
            def _():
                for i in range(W):
                    x_halo(e, 1 - side, i).wait_recv()

        y_halo(e, q).wait_recv()

    owner = [lax.div(slots[j], slot_dev) for j in range(n_snap)]

    def skipped(end, slot):
        if skips == 1:
            at = jnp.int32(0)
            for j in range(n_snap):
                at = jnp.where(slots[j] == slot, j, at)
            return (at,)
        low = jnp.int32(n_snap)
        high = jnp.int32(-1)
        for j in range(n_snap):
            low = jnp.where(owner[j] == end, jnp.minimum(low, j), low)
            high = jnp.where(owner[j] == end, j, high)
        return (low, high)

    not_up = skipped(n_probe - 1, n_probe * slot_dev - 1)
    not_down = skipped(0, 0)

    up_way = (up, up_send, up_recv, {"probe": z + 1}, z < n_probe - 1)
    down_way = (down, down_send, down_recv, {"probe": z - 1}, z > 0)

    def link(way, ref, s):
        return pltpu.make_async_remote_copy(
            src_ref=ref,
            dst_ref=ref,
            send_sem=way[1].at[lax.rem(s + lag, ring)],
            recv_sem=way[2].at[lax.rem(s + lag, ring)],
            device_id=way[3],
            device_id_type=MESH,
        )

    def send(way, ref, s):
        @pl.when(way[4] & (s >= ring - lag))
        def _():
            link(way, ref, s).wait_send()

        @pl.when(way[4])
        def _():
            link(way, ref, s).start()

    def relay(s, way, hops, step, missing):
        buf = way[0]
        head = lag * hops

        @pl.when(s < head)
        def _():
            group = lax.div(s, lag)
            item = s - group * lag
            w = lax.div(item, AHEAD)
            ref = first.at[(z - step * (group + 1)) * slot_dev + w, item - w * AHEAD]
            link(way, ref, s - lag).wait_recv()
            send(way, ref, s)

        k = s - head

        @pl.when((k >= 0) & (k < total))
        def _():
            m = lax.div(k, run)
            x = spot(AHEAD + k - m * run)
            position = m
            for place in missing:
                position = position + jnp.where(position >= place, 1, 0)
            slot = slots[position]
            mine = lax.div(slot, slot_dev) == z
            which = lax.rem(slot, slot_dev)

            @pl.when(hops == 0)
            def _():
                buf[k] = own[which, x]

            @pl.when(hops > 0)
            def _():
                link(way, buf.at[k], s - lag).wait_recv()
                buf[k] = lax.select(mine, own[which, x], buf[k])

            send(way, buf.at[k], s)

    def comm(s):
        relay(s, up_way, z, 1, not_up)
        relay(s, down_way, n_probe - 1 - z, -1, not_down)

    def fetch(j, q):
        @pl.when(q < AHEAD)
        def _():
            frames[j % 3, q] = first[slots[j], q]

        @pl.when(q >= AHEAD)
        def _():
            def pick(buf, missing):
                count = sum(jnp.where(place < j, 1, 0) for place in missing)
                found = None
                for d in range(skips + 1):
                    if 0 <= j - d < n_msg:
                        value = buf[(j - d) * run + q - AHEAD]
                        found = value if found is None else lax.select(count == d, value, found)
                return found

            from_up = owner[j] <= z
            for place in not_up:
                from_up = from_up & (place != j)
            frames[j % 3, q] = lax.select(from_up, pick(up, not_up), pick(down, not_down))

    weight = precond[ids[0]]

    def plane(n, q):
        a, b = n % 2, 1 - n % 2
        x = spot(q)
        if n > 0:
            halo_wait(n, q)
            halo_sent(n, q)
        if n == 0:
            fetch(0, q)
            fetch(1, q)
        fetch(n + 2, q)
        source = (
            frames[(n + 2) % 3, q].astype(jnp.float32)
            - 2.0 * frames[(n + 1) % 3, q].astype(jnp.float32)
            + frames[n % 3, q].astype(jnp.float32)
        )
        padded = field[a, x + W]
        high = padded.astype(jnp.bfloat16)
        low = (padded - high.astype(jnp.float32)).astype(jnp.bfloat16)
        lap = jnp.dot(
            ymat[...],
            jnp.concatenate([high, low, high], axis=0),
            preferred_element_type=jnp.float32,
        )
        high = high[PAD : PAD + ny]
        low = low[PAD : PAD + ny]
        lap = lap + jnp.dot(
            jnp.concatenate([high, low, high], axis=1),
            zmat[...],
            preferred_element_type=jnp.float32,
        )
        here = field[a, x + W, body_y]
        lap = lap + (3.0 * COEFFS[0]) * here
        for k in range(1, 5):
            lap = lap + COEFFS[k] * (field[a, x + W + k, body_y] + field[a, x + W - k, body_y])
        fresh = 2.0 * here - field[b, x + W, body_y] + cou[x] * lap - (weight * per[x]) * source
        if n == STEPS - 1:
            late[0, x] = fresh
            return
        field[b, x + W, body_y] = fresh
        halo_start(n + 1, q)
        if n == STEPS - 2:
            early[0, x] = fresh

    for item in range(lag):
        for way in (up_way, down_way):

            @pl.when(way[4])
            def _():
                ref = first.at[z * slot_dev + item // AHEAD, item % AHEAD]
                link(way, ref, item - lag).start()

    for load in loads[1:]:
        load.start()
    lead = lag * (n_probe - 1)
    loop(0, lead, comm)
    loads[1].wait()
    for side in range(2):

        @pl.when(sides[2 + side][0])
        def _():
            wide_halo(side).start()

    wide_halo(2).start()

    loop(lead, lead + 2 * run, comm)
    for load in loads[2:]:
        load.wait()
    for side in range(2):

        @pl.when(sides[2 + side][0])
        def _():
            wide_halo(side).wait_send()
            wide_halo(1 - side).wait_recv()

    wide_halo(2).wait()

    def comms(m, q):
        @pl.when((q >= AHEAD) & (q < nx))
        def _():
            comm(lead + m * run + q - AHEAD)

    for m in range(2, n_msg - 1):

        def simple(q, m=m):
            comms(m, q)
            plane(m - 2, q)

        loop(0, nx, simple)

    base = n_msg - 3
    levels = STEPS - base

    def done(level, q):
        if level == 0:
            return jnp.minimum(q, nx)
        w = 2 * W
        steady = q - w * level
        start = 2 * (q - w * level - w // 2)
        return jnp.clip(jnp.minimum(steady, start), 0, nx)

    def front(q):
        comms(n_msg - 1, q)
        for level in range(levels):
            loop(done(level, q), done(level, q + 1), functools.partial(plane, base + level))

    loop(0, nx + 2 * W * (levels - 1), front)

    def finish(s):
        for way in (up_way, down_way):

            @pl.when(way[4])
            def _():
                link(way, way[0].at[0], s).wait_send()

    loop(0, ring, finish)


def store(early, late, early_hbm, late_hbm, sem):
    depth = early.shape[1] // PARTS
    copies = [
        pltpu.make_async_copy(
            src.at[0, pl.ds(i * depth, depth)], dst.at[0, pl.ds(i * depth, depth)], sem.at[j, i]
        )
        for i in range(PARTS)
        for j, (src, dst) in enumerate(((early, early_hbm), (late, late_hbm)))
    ]
    for copy in copies:
        copy.start()
    for copy in copies:
        copy.wait()


def steps(
    sizes, skips, wave_prev, wave_cur, courant, perturb, snapshots, step_slots, precond, probe_ids
):
    nx, ny, nz = courant.shape
    slot_dev = snapshots.shape[0]
    total = (step_slots.shape[0] - skips) * (nx - AHEAD)
    ring = slot_dev * AHEAD * sizes[0]
    y_high, y_low = halves(band(ny, ny + 2 * PAD, PAD))
    z_high, z_low = halves(band(nz, nz, 0))
    ymat = jnp.asarray(np.concatenate([y_high, y_high, y_low], axis=1))
    zmat = jnp.asarray(np.concatenate([z_high, z_high, z_low], axis=0))
    smem = pl.BlockSpec(memory_space=pltpu.SMEM)
    vmem = pl.BlockSpec(memory_space=pltpu.VMEM)
    hbm = pl.BlockSpec(memory_space=pl.ANY)
    wave = pltpu.VMEM(wave_cur.shape, jnp.float32)
    dma = pltpu.SemaphoreType.DMA
    messages = pltpu.VMEM((total, ny, nz), jnp.bfloat16)
    results = pl.pallas_call(
        functools.partial(kernel, *sizes, skips),
        out_shape=(wave, wave),
        in_specs=[smem, smem, smem, vmem, vmem] + [hbm] * 5,
        out_specs=(vmem, vmem),
        scratch_shapes=[
            pltpu.VMEM((2, nx + 2 * W, ny + 2 * PAD, nz), jnp.float32),
            pltpu.VMEM((nx, ny, nz), jnp.float32),
            pltpu.VMEM((nx, ny, nz), jnp.float32),
            pltpu.VMEM((slot_dev, nx, ny, nz), jnp.bfloat16),
            pltpu.VMEM((sizes[0] * slot_dev, AHEAD, ny, nz), jnp.bfloat16),
            messages,
            messages,
            pltpu.VMEM((3, nx, ny, nz), jnp.bfloat16),
            dma((5,)),
            dma((ring,)),
            dma((ring,)),
            dma((ring,)),
            dma((ring,)),
            dma((3,)),
            dma((3,)),
            dma((2, W)),
            dma((2, 2, W)),
            dma((nx,)),
            dma((2, nx)),
        ],
        compiler_params=pltpu.CompilerParams(
            collective_id=skips - 1, has_side_effects=True, vmem_limit_bytes=54 * 1024 * 1024
        ),
    )(
        step_slots,
        precond,
        probe_ids,
        ymat,
        zmat,
        wave_prev,
        wave_cur,
        courant,
        perturb,
        snapshots,
    )
    return pl.pallas_call(
        store,
        out_shape=(jax.ShapeDtypeStruct(wave_cur.shape, jnp.float32),) * 2,
        in_specs=[vmem, vmem],
        out_specs=(hbm, hbm),
        scratch_shapes=[dma((2, PARTS))],
        compiler_params=pltpu.CompilerParams(vmem_limit_bytes=1024 * 1024),
    )(*results)


def shards(sizes, *args):
    snapshots, step_slots = args[4], args[5]
    n_probe, slot_dev = sizes[0], snapshots.shape[0]
    if slot_dev == 2:
        owner = step_slots // slot_dev
        ends = (jnp.sum(owner == 0) == slot_dev) & (jnp.sum(owner == n_probe - 1) == slot_dev)
        return lax.cond(
            ends,
            functools.partial(steps, sizes, 2),
            functools.partial(steps, sizes, 1),
            *args,
        )
    return steps(sizes, 1, *args)


def solution(mesh):
    placed = (
        P("probe", "gx", "gy", None),
        P("probe", "gx", "gy", None),
        P("gx", "gy", None),
        P("probe", "gx", "gy", None),
        P("probe", "gx", "gy", None),
        P(),
        P(),
        P("probe"),
    )
    sizes = (mesh.shape["probe"], mesh.shape["gx"], mesh.shape["gy"])
    return jax.shard_map(
        functools.partial(shards, sizes),
        mesh=mesh,
        in_specs=placed,
        out_specs=(P("probe", "gx", "gy", None), P("probe", "gx", "gy", None)),
        check_vma=False,
    )
```

```python
import functools

import jax
import jax.numpy as jnp
import ml_dtypes
import numpy as np
from jax import lax
from jax.experimental import pallas as pl
from jax.experimental.pallas import tpu as pltpu
from jax.sharding import PartitionSpec as P

STEPS = 4
COEFFS = (-205.0 / 72.0, 8.0 / 5.0, -1.0 / 5.0, 8.0 / 315.0, -1.0 / 560.0)
W = 4
PAD = 16
AHEAD = 2
PARTS = 4
MESH = pl.DeviceIdType.MESH


def band(rows, cols, shift):
    out = np.zeros((rows, cols), np.float64)
    for r in range(rows):
        for k in range(1, 5):
            for c in (r + shift - k, r + shift + k):
                if 0 <= c < cols:
                    out[r, c] += COEFFS[k]
    return out


def halves(matrix):
    high = matrix.astype(ml_dtypes.bfloat16)
    low = (matrix - high.astype(np.float64)).astype(ml_dtypes.bfloat16)
    return high, low


def kernel(
    n_probe,
    n_gx,
    n_gy,
    skips,
    need,
    slots,
    precond,
    ids,
    ymat,
    zmat,
    prev_hbm,
    cur_hbm,
    cou_hbm,
    per_hbm,
    snap_hbm,
    early,
    late,
    field,
    cou,
    per,
    own,
    first,
    up,
    down,
    frames,
    load_sem,
    up_send,
    up_recv,
    down_send,
    down_recv,
    wide_send,
    wide_recv,
    x_send,
    x_recv,
    y_send,
    y_recv,
):
    z = lax.axis_index("probe")
    gx = lax.axis_index("gx")
    gy = lax.axis_index("gy")
    nx, ny, nz = cou.shape
    slot_dev = own.shape[0]
    n_snap = slots.shape[0]
    n_msg = n_snap - skips
    run = nx - AHEAD
    total = n_msg * run
    lag = slot_dev * AHEAD
    ring = up_send.shape[0]
    body_x = pl.ds(W, nx)
    body_y = pl.ds(PAD, ny)

    def loop(low, high, fn):
        def step(i, carry):
            fn(i)
            return carry

        lax.fori_loop(low, high, step, 0)

    def spot(q):
        half = lax.div(q, 2)
        return jnp.where(lax.rem(q, 2) == 0, half, nx - 1 - half)

    loads = [
        pltpu.make_async_copy(snap_hbm, own, load_sem.at[0]),
        pltpu.make_async_copy(cur_hbm.at[0], field.at[0, body_x, body_y], load_sem.at[1]),
        pltpu.make_async_copy(prev_hbm.at[0], field.at[1, body_x, body_y], load_sem.at[2]),
        pltpu.make_async_copy(cou_hbm, cou, load_sem.at[3]),
        pltpu.make_async_copy(per_hbm.at[0], per, load_sem.at[4]),
    ]
    loads[0].start()

    zero_plane = jnp.zeros((ny, nz), jnp.float32)
    zero_rows = jnp.zeros((PAD, nz), jnp.float32)
    for b in range(2):
        for x in range(W):
            field[b, x, body_y] = zero_plane
            field[b, W + nx + x, body_y] = zero_plane

        def clear(x, b=b):
            field[b, W + x, pl.ds(0, PAD)] = zero_rows
            field[b, W + x, pl.ds(PAD + ny, PAD)] = zero_rows

        loop(0, nx, clear)

    sides = (
        (z < n_probe - 1, {"probe": z + 1}),
        (z > 0, {"probe": z - 1}),
        (gx < n_gx - 1, {"gx": gx + 1}),
        (gx > 0, {"gx": gx - 1}),
    )
    across = {"gy": 1 - gy}
    barrier = pltpu.get_barrier_semaphore()
    for there, target in sides:

        @pl.when(there)
        def _():
            pl.semaphore_signal(barrier, inc=1, device_id=target, device_id_type=MESH)

    pl.semaphore_signal(barrier, inc=1, device_id=across, device_id_type=MESH)
    loads[0].wait()
    for w in range(slot_dev):
        for q in range(AHEAD):
            first[z * slot_dev + w, q] = own[w, q // 2 if q % 2 == 0 else nx - 1 - q // 2]
    pl.semaphore_wait(barrier, 1 + sum(there.astype(jnp.int32) for there, _ in sides))

    y_from = pl.ds(pl.multiple_of(jnp.where(gy == 0, PAD + ny - 8, PAD), 8), 8)
    y_to = pl.ds(pl.multiple_of(jnp.where(gy == 0, PAD - 8, PAD + ny), 8), 8)

    def wide_halo(side):
        from_x, from_y, to_x, to_y = (
            (pl.ds(nx, W), body_y, pl.ds(0, W), body_y),
            (pl.ds(W, W), body_y, pl.ds(W + nx, W), body_y),
            (body_x, y_from, body_x, y_to),
        )[side]
        return pltpu.make_async_remote_copy(
            src_ref=field.at[0, from_x, from_y],
            dst_ref=field.at[0, to_x, to_y],
            send_sem=wide_send.at[side],
            recv_sem=wide_recv.at[side],
            device_id=across if side == 2 else sides[2 + side][1],
            device_id_type=MESH,
        )

    def x_halo(e, side, i):
        from_x = W + nx - 1 - i if side == 0 else W + i
        to_x = W - 1 - i if side == 0 else W + nx + i
        return pltpu.make_async_remote_copy(
            src_ref=field.at[e % 2, from_x, body_y],
            dst_ref=field.at[e % 2, to_x, body_y],
            send_sem=x_send.at[side, i],
            recv_sem=x_recv.at[e % 2, side, i],
            device_id=sides[2 + side][1],
            device_id_type=MESH,
        )

    def y_halo(e, q):
        x = W + spot(q)
        return pltpu.make_async_remote_copy(
            src_ref=field.at[e % 2, x, y_from],
            dst_ref=field.at[e % 2, x, y_to],
            send_sem=y_send.at[q],
            recv_sem=y_recv.at[e % 2, q],
            device_id=across,
            device_id_type=MESH,
        )

    def each_halo(e, q, act):
        for side in range(2):
            edge = (lax.rem(q, 2) == 1 - side) & (q < 2 * W)

            @pl.when(sides[2 + side][0] & edge)
            def _():
                act(x_halo(e, side, lax.div(q, 2)))

        act(y_halo(e, q))

    def halo_start(e, q):
        each_halo(e, q, lambda copy: copy.start())

    def halo_sent(e, q):
        each_halo(e, q, lambda copy: copy.wait_send())

    def halo_wait(e, q):
        for side in range(2):

            @pl.when(sides[2 + side][0] & (q == 0))
            def _():
                for i in range(W):
                    x_halo(e, 1 - side, i).wait_recv()

        y_halo(e, q).wait_recv()

    owner = [lax.div(slots[j], slot_dev) for j in range(n_snap)]

    def skipped(end, slot):
        if skips == 1:
            at = jnp.int32(0)
            for j in range(n_snap):
                at = jnp.where(slots[j] == slot, j, at)
            return (at,)
        low = jnp.int32(n_snap)
        high = jnp.int32(-1)
        for j in range(n_snap):
            low = jnp.where(owner[j] == end, jnp.minimum(low, j), low)
            high = jnp.where(owner[j] == end, j, high)
        return (low, high)

    not_up = skipped(n_probe - 1, n_probe * slot_dev - 1)
    not_down = skipped(0, 0)

    up_way = (up, up_send, up_recv, {"probe": z + 1}, z < n_probe - 1)
    down_way = (down, down_send, down_recv, {"probe": z - 1}, z > 0)

    def link(way, ref, s):
        return pltpu.make_async_remote_copy(
            src_ref=ref,
            dst_ref=ref,
            send_sem=way[1].at[lax.rem(s + lag, ring)],
            recv_sem=way[2].at[lax.rem(s + lag, ring)],
            device_id=way[3],
            device_id_type=MESH,
        )

    def send(way, ref, s):
        @pl.when(way[4] & (s >= ring - lag))
        def _():
            link(way, ref, s).wait_send()

        @pl.when(way[4])
        def _():
            link(way, ref, s).start()

    def relay(s, way, hops, step, missing):
        buf = way[0]
        head = lag * hops

        @pl.when(s < head)
        def _():
            group = lax.div(s, lag)
            item = s - group * lag
            w = lax.div(item, AHEAD)
            ref = first.at[(z - step * (group + 1)) * slot_dev + w, item - w * AHEAD]
            link(way, ref, s - lag).wait_recv()
            send(way, ref, s)

        k = s - head

        @pl.when((k >= 0) & (k < total))
        def _():
            m = lax.div(k, run)
            x = spot(AHEAD + k - m * run)
            position = m
            for place in missing:
                position = position + jnp.where(position >= place, 1, 0)
            slot = slots[position]
            mine = lax.div(slot, slot_dev) == z
            which = lax.rem(slot, slot_dev)

            @pl.when(hops == 0)
            def _():
                buf[k] = own[which, x]

            @pl.when(hops > 0)
            def _():
                link(way, buf.at[k], s - lag).wait_recv()
                buf[k] = lax.select(mine, own[which, x], buf[k])

            send(way, buf.at[k], s)

    def comm(s):
        relay(s, up_way, z, 1, not_up)
        relay(s, down_way, n_probe - 1 - z, -1, not_down)

    def fetch(j, q):
        @pl.when(q < AHEAD)
        def _():
            frames[j % 3, q] = first[slots[j], q]

        @pl.when(q >= AHEAD)
        def _():
            def pick(buf, missing):
                count = sum(jnp.where(place < j, 1, 0) for place in missing)
                found = None
                for d in range(skips + 1):
                    if 0 <= j - d <= need[j]:
                        value = buf[(j - d) * run + q - AHEAD]
                        found = value if found is None else lax.select(count == d, value, found)
                return found

            from_up = owner[j] <= z
            for place in not_up:
                from_up = from_up & (place != j)
            frames[j % 3, q] = lax.select(from_up, pick(up, not_up), pick(down, not_down))

    weight = precond[ids[0]]

    def plane(n, q):
        a, b = n % 2, 1 - n % 2
        x = spot(q)
        if n > 0:
            halo_wait(n, q)
            halo_sent(n, q)
        if n == 0:
            fetch(0, q)
            fetch(1, q)
        fetch(n + 2, q)
        source = (
            frames[(n + 2) % 3, q].astype(jnp.float32)
            - 2.0 * frames[(n + 1) % 3, q].astype(jnp.float32)
            + frames[n % 3, q].astype(jnp.float32)
        )
        padded = field[a, x + W]
        high = padded.astype(jnp.bfloat16)
        low = (padded - high.astype(jnp.float32)).astype(jnp.bfloat16)
        lap = jnp.dot(
            ymat[...],
            jnp.concatenate([high, low, high], axis=0),
            preferred_element_type=jnp.float32,
        )
        high = high[PAD : PAD + ny]
        low = low[PAD : PAD + ny]
        lap = lap + jnp.dot(
            jnp.concatenate([high, low, high], axis=1),
            zmat[...],
            preferred_element_type=jnp.float32,
        )
        here = field[a, x + W, body_y]
        lap = lap + (3.0 * COEFFS[0]) * here
        for k in range(1, 5):
            lap = lap + COEFFS[k] * (field[a, x + W + k, body_y] + field[a, x + W - k, body_y])
        fresh = 2.0 * here - field[b, x + W, body_y] + cou[x] * lap - (weight * per[x]) * source
        if n == STEPS - 1:
            late[0, x] = fresh
            return
        field[b, x + W, body_y] = fresh
        halo_start(n + 1, q)
        if n == STEPS - 2:
            early[0, x] = fresh

    for item in range(lag):
        for way in (up_way, down_way):

            @pl.when(way[4])
            def _():
                ref = first.at[z * slot_dev + item // AHEAD, item % AHEAD]
                link(way, ref, item - lag).start()

    for load in loads[1:]:
        load.start()
    lead = lag * (n_probe - 1)
    loop(0, lead, comm)
    loads[1].wait()
    for side in range(2):

        @pl.when(sides[2 + side][0])
        def _():
            wide_halo(side).start()

    wide_halo(2).start()

    loop(lead, lead + 2 * run, comm)
    for load in loads[2:]:
        load.wait()
    for side in range(2):

        @pl.when(sides[2 + side][0])
        def _():
            wide_halo(side).wait_send()
            wide_halo(1 - side).wait_recv()

    wide_halo(2).wait()

    lags = [0]
    for n in range(1, STEPS):
        lags.append(lags[-1] + 2 * W if need[n + 2] == need[n + 1] else 0)

    def done(n, g):
        ahead = g - nx * need[n + 2] - lags[n]
        if lags[n]:
            ahead = jnp.minimum(ahead, 2 * (ahead - W))
        return jnp.clip(ahead, 0, nx)

    def turn(g):
        m = lax.div(g, nx)
        q = g - m * nx

        @pl.when((q >= AHEAD) & (m < n_msg))
        def _():
            comm(lead + m * run + q - AHEAD)

        for n in range(STEPS):
            loop(done(n, g), done(n, g + 1), functools.partial(plane, n))

    loop(2 * nx, nx * n_msg + max(0, lags[-1]), turn)

    def finish(s):
        for way in (up_way, down_way):

            @pl.when(way[4])
            def _():
                link(way, way[0].at[0], s).wait_send()

    loop(0, ring, finish)


def store(early, late, early_hbm, late_hbm, sem):
    depth = early.shape[1] // PARTS
    copies = [
        pltpu.make_async_copy(
            src.at[0, pl.ds(i * depth, depth)], dst.at[0, pl.ds(i * depth, depth)], sem.at[j, i]
        )
        for i in range(PARTS)
        for j, (src, dst) in enumerate(((early, early_hbm), (late, late_hbm)))
    ]
    for copy in copies:
        copy.start()
    for copy in copies:
        copy.wait()


def steps(
    sizes, ident, skips, need, wave_prev, wave_cur, courant, perturb, snapshots, step_slots, precond, probe_ids
):
    nx, ny, nz = courant.shape
    slot_dev = snapshots.shape[0]
    total = (step_slots.shape[0] - skips) * (nx - AHEAD)
    ring = slot_dev * AHEAD * sizes[0]
    y_high, y_low = halves(band(ny, ny + 2 * PAD, PAD))
    z_high, z_low = halves(band(nz, nz, 0))
    ymat = jnp.asarray(np.concatenate([y_high, y_high, y_low], axis=1))
    zmat = jnp.asarray(np.concatenate([z_high, z_high, z_low], axis=0))
    smem = pl.BlockSpec(memory_space=pltpu.SMEM)
    vmem = pl.BlockSpec(memory_space=pltpu.VMEM)
    hbm = pl.BlockSpec(memory_space=pl.ANY)
    wave = pltpu.VMEM(wave_cur.shape, jnp.float32)
    dma = pltpu.SemaphoreType.DMA
    messages = pltpu.VMEM((total, ny, nz), jnp.bfloat16)
    results = pl.pallas_call(
        functools.partial(kernel, *sizes, skips, need),
        out_shape=(wave, wave),
        in_specs=[smem, smem, smem, vmem, vmem] + [hbm] * 5,
        out_specs=(vmem, vmem),
        scratch_shapes=[
            pltpu.VMEM((2, nx + 2 * W, ny + 2 * PAD, nz), jnp.float32),
            pltpu.VMEM((nx, ny, nz), jnp.float32),
            pltpu.VMEM((nx, ny, nz), jnp.float32),
            pltpu.VMEM((slot_dev, nx, ny, nz), jnp.bfloat16),
            pltpu.VMEM((sizes[0] * slot_dev, AHEAD, ny, nz), jnp.bfloat16),
            messages,
            messages,
            pltpu.VMEM((3, nx, ny, nz), jnp.bfloat16),
            dma((5,)),
            dma((ring,)),
            dma((ring,)),
            dma((ring,)),
            dma((ring,)),
            dma((3,)),
            dma((3,)),
            dma((2, W)),
            dma((2, 2, W)),
            dma((nx,)),
            dma((2, nx)),
        ],
        compiler_params=pltpu.CompilerParams(
            collective_id=ident, has_side_effects=True, vmem_limit_bytes=54 * 1024 * 1024
        ),
    )(
        step_slots,
        precond,
        probe_ids,
        ymat,
        zmat,
        wave_prev,
        wave_cur,
        courant,
        perturb,
        snapshots,
    )
    return pl.pallas_call(
        store,
        out_shape=(jax.ShapeDtypeStruct(wave_cur.shape, jnp.float32),) * 2,
        in_specs=[vmem, vmem],
        out_specs=(hbm, hbm),
        scratch_shapes=[dma((2, PARTS))],
        compiler_params=pltpu.CompilerParams(vmem_limit_bytes=1024 * 1024),
    )(*results)


def choose(top, slots, pick):
    at = [slots[j] for j in range(slots.shape[0])]
    one = lambda flag: jnp.where(flag, 1, 0)
    side = [one(a < 2) + 2 * one(a > top - 2) for a in at]
    ends = sum(one(s > 0) for s in side)
    fixed = one((at[-1] == 0) | (at[-1] == top))
    four = 2 + one(side[-1] > 0) * (1 + one(side[-2] == side[-1]))
    pick[0] = jnp.where(ends == 4, four, fixed)


def shards(sizes, *args):
    snapshots, step_slots = args[4], args[5]
    n_probe, slot_dev = sizes[0], snapshots.shape[0]
    n_snap = step_slots.shape[0]

    def plan(skips):
        return tuple(min(j, n_snap - skips - 1) for j in range(n_snap))

    if slot_dev != 2 or n_snap != 6:
        return steps(sizes, 0, 1, plan(1), *args)
    smem = pl.BlockSpec(memory_space=pltpu.SMEM)
    pick = pl.pallas_call(
        functools.partial(choose, n_probe * slot_dev - 1),
        out_shape=pltpu.SMEM((1,), jnp.int32),
        in_specs=[smem],
        out_specs=smem,
    )(step_slots)
    plans = (
        (1, (0, 1, 2, 3, 3, 4)),
        (1, plan(1)),
        (2, (0, 1, 2, 2, 2, 3)),
        (2, (0, 1, 2, 2, 3, 3)),
        (2, plan(2)),
    )
    ways = [functools.partial(steps, sizes, i, *p) for i, p in enumerate(plans)]
    return lax.switch(pick[0], ways, *args)


def solution(mesh):
    placed = (
        P("probe", "gx", "gy", None),
        P("probe", "gx", "gy", None),
        P("gx", "gy", None),
        P("probe", "gx", "gy", None),
        P("probe", "gx", "gy", None),
        P(),
        P(),
        P("probe"),
    )
    sizes = (mesh.shape["probe"], mesh.shape["gx"], mesh.shape["gy"])
    return jax.shard_map(
        functools.partial(shards, sizes),
        mesh=mesh,
        in_specs=placed,
        out_specs=(P("probe", "gx", "gy", None), P("probe", "gx", "gy", None)),
        check_vma=False,
    )
```

```python
import functools

import jax
import jax.numpy as jnp
import ml_dtypes
import numpy as np
from jax import lax
from jax.experimental import pallas as pl
from jax.experimental.pallas import tpu as pltpu
from jax.sharding import PartitionSpec as P

STEPS = 4
COEFFS = (-205.0 / 72.0, 8.0 / 5.0, -1.0 / 5.0, 8.0 / 315.0, -1.0 / 560.0)
W = 4
PAD = 16
AHEAD = 2
PARTS = 4
MESH = pl.DeviceIdType.MESH


def band(rows, cols, shift):
    out = np.zeros((rows, cols), np.float64)
    for r in range(rows):
        for k in range(1, 5):
            for c in (r + shift - k, r + shift + k):
                if 0 <= c < cols:
                    out[r, c] += COEFFS[k]
    return out


def halves(matrix):
    high = matrix.astype(ml_dtypes.bfloat16)
    low = (matrix - high.astype(np.float64)).astype(ml_dtypes.bfloat16)
    return high, low


def kernel(
    n_probe,
    n_gx,
    n_gy,
    skips,
    need,
    slots,
    precond,
    ids,
    ymat_hbm,
    zmat_hbm,
    prev_hbm,
    cur_hbm,
    cou_hbm,
    per_hbm,
    snap_hbm,
    early,
    late,
    ymat,
    zmat,
    field,
    cou,
    per,
    own,
    first,
    up,
    down,
    frames,
    load_sem,
    up_send,
    up_recv,
    down_send,
    down_recv,
    wide_send,
    wide_recv,
    x_send,
    x_recv,
    y_send,
    y_recv,
):
    z = lax.axis_index("probe")
    gx = lax.axis_index("gx")
    gy = lax.axis_index("gy")
    nx, ny, nz = cou.shape
    slot_dev = own.shape[0]
    n_snap = slots.shape[0]
    n_msg = n_snap - skips
    run = nx - AHEAD
    total = n_msg * run
    lag = slot_dev * AHEAD
    ring = up_send.shape[0]
    body_x = pl.ds(W, nx)
    body_y = pl.ds(PAD, ny)

    def loop(low, high, fn):
        def step(i, carry):
            fn(i)
            return carry

        lax.fori_loop(low, high, step, 0)

    def spot(q):
        half = lax.div(q, 2)
        return jnp.where(lax.rem(q, 2) == 0, half, nx - 1 - half)

    loads = [
        pltpu.make_async_copy(snap_hbm, own, load_sem.at[0]),
        pltpu.make_async_copy(cur_hbm.at[0], field.at[0, body_x, body_y], load_sem.at[1]),
        pltpu.make_async_copy(prev_hbm.at[0], field.at[1, body_x, body_y], load_sem.at[2]),
        pltpu.make_async_copy(cou_hbm, cou, load_sem.at[3]),
        pltpu.make_async_copy(per_hbm.at[0], per, load_sem.at[4]),
        pltpu.make_async_copy(ymat_hbm, ymat, load_sem.at[5]),
        pltpu.make_async_copy(zmat_hbm, zmat, load_sem.at[6]),
    ]
    heads = [
        pltpu.make_async_copy(
            snap_hbm.at[w, q // 2 if q % 2 == 0 else nx - 1 - q // 2],
            first.at[z * slot_dev + w, q],
            load_sem.at[7 + w * AHEAD + q],
        )
        for w in range(slot_dev)
        for q in range(AHEAD)
    ]
    for head in heads:
        head.start()

    loads[0].start()

    sides = (
        (z < n_probe - 1, {"probe": z + 1}),
        (z > 0, {"probe": z - 1}),
        (gx < n_gx - 1, {"gx": gx + 1}),
        (gx > 0, {"gx": gx - 1}),
    )
    across = {"gy": 1 - gy}
    barrier = pltpu.get_barrier_semaphore()
    for there, target in sides:

        @pl.when(there)
        def _():
            pl.semaphore_signal(barrier, inc=1, device_id=target, device_id_type=MESH)

    pl.semaphore_signal(barrier, inc=1, device_id=across, device_id_type=MESH)
    for head in heads:
        head.wait()

    pl.semaphore_wait(barrier, 1 + sum(there.astype(jnp.int32) for there, _ in sides))

    y_from = pl.ds(pl.multiple_of(jnp.where(gy == 0, PAD + ny - 8, PAD), 8), 8)
    y_to = pl.ds(pl.multiple_of(jnp.where(gy == 0, PAD - 8, PAD + ny), 8), 8)

    def wide_halo(side):
        from_x, from_y, to_x, to_y = (
            (pl.ds(nx, W), body_y, pl.ds(0, W), body_y),
            (pl.ds(W, W), body_y, pl.ds(W + nx, W), body_y),
            (body_x, y_from, body_x, y_to),
        )[side]
        return pltpu.make_async_remote_copy(
            src_ref=field.at[0, from_x, from_y],
            dst_ref=field.at[0, to_x, to_y],
            send_sem=wide_send.at[side],
            recv_sem=wide_recv.at[side],
            device_id=across if side == 2 else sides[2 + side][1],
            device_id_type=MESH,
        )

    def x_halo(e, side, i):
        from_x = W + nx - 1 - i if side == 0 else W + i
        to_x = W - 1 - i if side == 0 else W + nx + i
        return pltpu.make_async_remote_copy(
            src_ref=field.at[e % 2, from_x, body_y],
            dst_ref=field.at[e % 2, to_x, body_y],
            send_sem=x_send.at[side, i],
            recv_sem=x_recv.at[e % 2, side, i],
            device_id=sides[2 + side][1],
            device_id_type=MESH,
        )

    def y_halo(e, q):
        x = W + spot(q)
        return pltpu.make_async_remote_copy(
            src_ref=field.at[e % 2, x, y_from],
            dst_ref=field.at[e % 2, x, y_to],
            send_sem=y_send.at[q],
            recv_sem=y_recv.at[e % 2, q],
            device_id=across,
            device_id_type=MESH,
        )

    def each_halo(e, q, act):
        for side in range(2):
            edge = (lax.rem(q, 2) == 1 - side) & (q < 2 * W)

            @pl.when(sides[2 + side][0] & edge)
            def _():
                act(x_halo(e, side, lax.div(q, 2)))

        act(y_halo(e, q))

    def halo_start(e, q):
        each_halo(e, q, lambda copy: copy.start())

    def halo_sent(e, q):
        each_halo(e, q, lambda copy: copy.wait_send())

    def halo_wait(e, q):
        for side in range(2):

            @pl.when(sides[2 + side][0] & (q == 0))
            def _():
                for i in range(W):
                    x_halo(e, 1 - side, i).wait_recv()

        y_halo(e, q).wait_recv()

    owner = [lax.div(slots[j], slot_dev) for j in range(n_snap)]

    def skipped(end):
        low = jnp.int32(n_snap)
        high = jnp.int32(-1)
        for j in range(n_snap):
            low = jnp.where(owner[j] == end, jnp.minimum(low, j), low)
            high = jnp.where(owner[j] == end, j, high)
        return (low, high)[:skips]

    not_up = skipped(n_probe - 1)
    not_down = skipped(0)

    up_way = (up, up_send, up_recv, {"probe": z + 1}, z < n_probe - 1)
    down_way = (down, down_send, down_recv, {"probe": z - 1}, z > 0)

    def link(way, ref, s):
        return pltpu.make_async_remote_copy(
            src_ref=ref,
            dst_ref=ref,
            send_sem=way[1].at[lax.rem(s + lag, ring)],
            recv_sem=way[2].at[lax.rem(s + lag, ring)],
            device_id=way[3],
            device_id_type=MESH,
        )

    def send(way, ref, s):
        @pl.when(way[4] & (s >= ring - lag))
        def _():
            link(way, ref, s).wait_send()

        @pl.when(way[4])
        def _():
            link(way, ref, s).start()

    def relay(s, way, hops, step, missing):
        buf = way[0]
        head = lag * hops

        @pl.when(s < head)
        def _():
            group = lax.div(s, lag)
            item = s - group * lag
            w = lax.div(item, AHEAD)
            ref = first.at[(z - step * (group + 1)) * slot_dev + w, item - w * AHEAD]
            link(way, ref, s - lag).wait_recv()
            send(way, ref, s)

        k = s - head

        @pl.when((k >= 0) & (k < total))
        def _():
            m = lax.div(k, run)
            x = spot(AHEAD + k - m * run)
            position = m
            for place in missing:
                position = position + jnp.where(position >= place, 1, 0)
            slot = slots[position]
            mine = lax.div(slot, slot_dev) == z
            which = lax.rem(slot, slot_dev)

            @pl.when(hops == 0)
            def _():
                buf[k] = own[which, x]

            @pl.when(hops > 0)
            def _():
                link(way, buf.at[k], s - lag).wait_recv()
                buf[k] = lax.select(mine, own[which, x], buf[k])

            send(way, buf.at[k], s)

    def comm(s):
        relay(s, up_way, z, 1, not_up)
        relay(s, down_way, n_probe - 1 - z, -1, not_down)

    def fetch(j, q):
        @pl.when(q < AHEAD)
        def _():
            frames[j % 3, q] = first[slots[j], q]

        @pl.when(q >= AHEAD)
        def _():
            def pick(buf, missing):
                count = sum(jnp.where(place < j, 1, 0) for place in missing)
                found = None
                for d in range(skips + 1):
                    if 0 <= j - d <= need[j]:
                        value = buf[(j - d) * run + q - AHEAD]
                        found = value if found is None else lax.select(count == d, value, found)
                return found

            from_up = owner[j] <= z
            for place in not_up:
                from_up = from_up & (place != j)
            frames[j % 3, q] = lax.select(from_up, pick(up, not_up), pick(down, not_down))

    weight = precond[ids[0]]

    def plane(n, q):
        a, b = n % 2, 1 - n % 2
        x = spot(q)
        if n > 0:
            halo_wait(n, q)
            halo_sent(n, q)
        if n == 0:
            fetch(0, q)
            fetch(1, q)
        fetch(n + 2, q)
        source = (
            frames[(n + 2) % 3, q].astype(jnp.float32)
            - 2.0 * frames[(n + 1) % 3, q].astype(jnp.float32)
            + frames[n % 3, q].astype(jnp.float32)
        )
        padded = field[a, x + W]
        high = padded.astype(jnp.bfloat16)
        low = (padded - high.astype(jnp.float32)).astype(jnp.bfloat16)
        lap = jnp.dot(
            ymat[...],
            jnp.concatenate([high, low, high], axis=0),
            preferred_element_type=jnp.float32,
        )
        high = high[PAD : PAD + ny]
        low = low[PAD : PAD + ny]
        lap = lap + jnp.dot(
            jnp.concatenate([high, low, high], axis=1),
            zmat[...],
            preferred_element_type=jnp.float32,
        )
        here = field[a, x + W, body_y]
        lap = lap + (3.0 * COEFFS[0]) * here
        for k in range(1, 5):
            lap = lap + COEFFS[k] * (field[a, x + W + k, body_y] + field[a, x + W - k, body_y])
        fresh = 2.0 * here - field[b, x + W, body_y] + cou[x] * lap - (weight * per[x]) * source
        if n == STEPS - 1:
            late[0, x] = fresh
            return
        field[b, x + W, body_y] = fresh
        halo_start(n + 1, q)
        if n == STEPS - 2:
            early[0, x] = fresh

    for item in range(lag):
        for way in (up_way, down_way):

            @pl.when(way[4])
            def _():
                ref = first.at[z * slot_dev + item // AHEAD, item % AHEAD]
                link(way, ref, item - lag).start()

    for load in loads[1:]:
        load.start()

    zero_plane = jnp.zeros((ny, nz), jnp.float32)
    zero_rows = jnp.zeros((8, nz), jnp.float32)
    shut = pl.ds(pl.multiple_of(jnp.where(gy == 0, PAD - 8, PAD + ny), 8), 8)
    for b in range(2):
        for end, x in ((n_gx - 1, W + nx), (0, 0)):

            @pl.when(gx == end)
            def _():
                for i in range(W):
                    field[b, x + i, body_y] = zero_plane

        def clear(x, b=b):
            for part in (pl.ds(0, PAD - 8), pl.ds(PAD + ny + 8, PAD - 8), shut):
                field[b, W + x, part] = zero_rows

        loop(0, nx, clear)

    loads[0].wait()
    lead = lag * (n_probe - 1)
    loop(0, lead, comm)
    loads[1].wait()
    for side in range(2):

        @pl.when(sides[2 + side][0])
        def _():
            wide_halo(side).start()

    wide_halo(2).start()

    loop(lead, lead + 2 * run, comm)
    for load in loads[2:]:
        load.wait()
    for side in range(2):

        @pl.when(sides[2 + side][0])
        def _():
            wide_halo(side).wait_send()
            wide_halo(1 - side).wait_recv()

    wide_halo(2).wait()

    lags = [0]
    for n in range(1, STEPS):
        lags.append(lags[-1] + 2 * W if need[n + 2] == need[n + 1] else 0)

    def done(n, g):
        ahead = g - nx * need[n + 2] - lags[n]
        if lags[n]:
            ahead = jnp.minimum(ahead, 2 * (ahead - W))
        return jnp.clip(ahead, 0, nx)

    def turn(g):
        m = lax.div(g, nx)
        q = g - m * nx

        @pl.when((q >= AHEAD) & (m < n_msg))
        def _():
            comm(lead + m * run + q - AHEAD)

        for n in range(STEPS):
            loop(done(n, g), done(n, g + 1), functools.partial(plane, n))

    loop(2 * nx, nx * n_msg + max(0, lags[-1]), turn)

    def finish(s):
        for way in (up_way, down_way):

            @pl.when(way[4])
            def _():
                link(way, way[0].at[0], s).wait_send()

    loop(0, ring, finish)


def store(early, late, early_hbm, late_hbm, sem):
    depth = early.shape[1] // PARTS
    copies = [
        pltpu.make_async_copy(
            src.at[0, pl.ds(i * depth, depth)], dst.at[0, pl.ds(i * depth, depth)], sem.at[j, i]
        )
        for i in range(PARTS)
        for j, (src, dst) in enumerate(((early, early_hbm), (late, late_hbm)))
    ]
    for copy in copies:
        copy.start()
    for copy in copies:
        copy.wait()


def steps(
    sizes, ident, skips, need, wave_prev, wave_cur, courant, perturb, snapshots, step_slots, precond, probe_ids
):
    nx, ny, nz = courant.shape
    slot_dev = snapshots.shape[0]
    total = (step_slots.shape[0] - skips) * (nx - AHEAD)
    ring = slot_dev * AHEAD * sizes[0]
    y_high, y_low = halves(band(ny, ny + 2 * PAD, PAD))
    z_high, z_low = halves(band(nz, nz, 0))
    ymat = jnp.asarray(np.concatenate([y_high, y_high, y_low], axis=1))
    zmat = jnp.asarray(np.concatenate([z_high, z_high, z_low], axis=0))
    smem = pl.BlockSpec(memory_space=pltpu.SMEM)
    vmem = pl.BlockSpec(memory_space=pltpu.VMEM)
    hbm = pl.BlockSpec(memory_space=pl.ANY)
    wave = pltpu.VMEM(wave_cur.shape, jnp.float32)
    dma = pltpu.SemaphoreType.DMA
    messages = pltpu.VMEM((total, ny, nz), jnp.bfloat16)
    results = pl.pallas_call(
        functools.partial(kernel, *sizes, skips, need),
        out_shape=(wave, wave),
        in_specs=[smem] * 3 + [hbm] * 7,
        out_specs=(vmem, vmem),
        scratch_shapes=[
            pltpu.VMEM(ymat.shape, jnp.bfloat16),
            pltpu.VMEM(zmat.shape, jnp.bfloat16),
            pltpu.VMEM((2, nx + 2 * W, ny + 2 * PAD, nz), jnp.float32),
            pltpu.VMEM((nx, ny, nz), jnp.float32),
            pltpu.VMEM((nx, ny, nz), jnp.float32),
            pltpu.VMEM((slot_dev, nx, ny, nz), jnp.bfloat16),
            pltpu.VMEM((sizes[0] * slot_dev, AHEAD, ny, nz), jnp.bfloat16),
            messages,
            messages,
            pltpu.VMEM((3, nx, ny, nz), jnp.bfloat16),
            dma((7 + slot_dev * AHEAD,)),
            dma((ring,)),
            dma((ring,)),
            dma((ring,)),
            dma((ring,)),
            dma((3,)),
            dma((3,)),
            dma((2, W)),
            dma((2, 2, W)),
            dma((nx,)),
            dma((2, nx)),
        ],
        compiler_params=pltpu.CompilerParams(
            collective_id=ident, has_side_effects=True, vmem_limit_bytes=54 * 1024 * 1024
        ),
    )(
        step_slots,
        precond,
        probe_ids,
        ymat,
        zmat,
        wave_prev,
        wave_cur,
        courant,
        perturb,
        snapshots,
    )
    return pl.pallas_call(
        store,
        out_shape=(jax.ShapeDtypeStruct(wave_cur.shape, jnp.float32),) * 2,
        in_specs=[vmem, vmem],
        out_specs=(hbm, hbm),
        scratch_shapes=[dma((2, PARTS))],
        compiler_params=pltpu.CompilerParams(vmem_limit_bytes=1024 * 1024),
    )(*results)


def choose(top, slots, pick):
    at = [slots[j] for j in range(slots.shape[0])]
    one = lambda flag: jnp.where(flag, 1, 0)
    side = [one(a < 2) + 2 * one(a > top - 2) for a in at]
    ends = sum(one(s > 0) for s in side)
    alone = sum(one(s == side[-1]) for s in side) == 1
    fixed = one((side[-1] > 0) & alone)
    four = 2 + one(side[-1] > 0) * (1 + one(side[-2] == side[-1]))
    pick[0] = jnp.where(ends == 4, four, fixed)


def shards(sizes, *args):
    snapshots, step_slots = args[4], args[5]
    n_probe, slot_dev = sizes[0], snapshots.shape[0]
    n_snap = step_slots.shape[0]

    def plan(skips):
        return tuple(min(j, n_snap - skips - 1) for j in range(n_snap))

    if slot_dev != 2 or n_snap != 6:
        return steps(sizes, 0, 1, plan(1), *args)
    smem = pl.BlockSpec(memory_space=pltpu.SMEM)
    pick = pl.pallas_call(
        functools.partial(choose, n_probe * slot_dev - 1),
        out_shape=pltpu.SMEM((1,), jnp.int32),
        in_specs=[smem],
        out_specs=smem,
    )(step_slots)
    plans = (
        (1, (0, 1, 2, 3, 3, 4)),
        (1, plan(1)),
        (2, (0, 1, 2, 2, 2, 3)),
        (2, (0, 1, 2, 2, 3, 3)),
        (2, plan(2)),
    )
    ways = [functools.partial(steps, sizes, i, *p) for i, p in enumerate(plans)]
    return lax.switch(pick[0], ways, *args)


def solution(mesh):
    placed = (
        P("probe", "gx", "gy", None),
        P("probe", "gx", "gy", None),
        P("gx", "gy", None),
        P("probe", "gx", "gy", None),
        P("probe", "gx", "gy", None),
        P(),
        P(),
        P("probe"),
    )
    sizes = (mesh.shape["probe"], mesh.shape["gx"], mesh.shape["gy"])
    return jax.shard_map(
        functools.partial(shards, sizes),
        mesh=mesh,
        in_specs=placed,
        out_specs=(P("probe", "gx", "gy", None), P("probe", "gx", "gy", None)),
        check_vma=False,
    )
```

```python
import functools

import jax
import jax.numpy as jnp
import ml_dtypes
import numpy as np
from jax import lax
from jax.experimental import pallas as pl
from jax.experimental.pallas import tpu as pltpu
from jax.sharding import PartitionSpec as P

STEPS = 4
COEFFS = (-205.0 / 72.0, 8.0 / 5.0, -1.0 / 5.0, 8.0 / 315.0, -1.0 / 560.0)
W = 4
PAD = 16
AHEAD = 2
PARTS = 4
MESH = pl.DeviceIdType.MESH


def band(rows, cols, shift):
    out = np.zeros((rows, cols), np.float64)
    for r in range(rows):
        for k in range(1, 5):
            for c in (r + shift - k, r + shift + k):
                if 0 <= c < cols:
                    out[r, c] += COEFFS[k]
    return out


def halves(matrix):
    high = matrix.astype(ml_dtypes.bfloat16)
    low = (matrix - high.astype(np.float64)).astype(ml_dtypes.bfloat16)
    return high, low


def kernel(
    n_probe,
    n_gx,
    n_gy,
    skips,
    need,
    slots,
    precond,
    ids,
    ymat_hbm,
    zmat_hbm,
    prev_hbm,
    cur_hbm,
    cou_hbm,
    per_hbm,
    snap_hbm,
    early,
    late,
    ymat,
    zmat,
    field,
    cou,
    per,
    own,
    first,
    up,
    down,
    frames,
    load_sem,
    up_send,
    up_recv,
    down_send,
    down_recv,
    wide_send,
    wide_recv,
    x_send,
    x_recv,
    y_send,
    y_recv,
):
    z = lax.axis_index("probe")
    gx = lax.axis_index("gx")
    gy = lax.axis_index("gy")
    nx, ny, nz = cou.shape
    slot_dev = own.shape[0]
    n_snap = slots.shape[0]
    n_msg = n_snap - skips
    run = nx - AHEAD
    total = n_msg * run
    lag = slot_dev * AHEAD
    ring = up_send.shape[0]
    body_x = pl.ds(W, nx)
    body_y = pl.ds(PAD, ny)

    def loop(low, high, fn):
        def step(i, carry):
            fn(i)
            return carry

        lax.fori_loop(low, high, step, 0)

    def spot(q):
        half = lax.div(q, 2)
        return jnp.where(lax.rem(q, 2) == 0, half, nx - 1 - half)

    sides = (
        (z < n_probe - 1, {"probe": z + 1}),
        (z > 0, {"probe": z - 1}),
        (gx < n_gx - 1, {"gx": gx + 1}),
        (gx > 0, {"gx": gx - 1}),
    )
    across = {"gy": 1 - gy}
    barrier = pltpu.get_barrier_semaphore()
    for there, target in sides:

        @pl.when(there)
        def _():
            pl.semaphore_signal(barrier, inc=1, device_id=target, device_id_type=MESH)

    pl.semaphore_signal(barrier, inc=1, device_id=across, device_id_type=MESH)
    loads = [
        pltpu.make_async_copy(snap_hbm, own, load_sem.at[0]),
        pltpu.make_async_copy(cur_hbm.at[0], field.at[0, body_x, body_y], load_sem.at[1]),
        pltpu.make_async_copy(prev_hbm.at[0], field.at[1, body_x, body_y], load_sem.at[2]),
        pltpu.make_async_copy(cou_hbm, cou, load_sem.at[3]),
        pltpu.make_async_copy(per_hbm.at[0], per, load_sem.at[4]),
        pltpu.make_async_copy(ymat_hbm, ymat, load_sem.at[5]),
        pltpu.make_async_copy(zmat_hbm, zmat, load_sem.at[6]),
    ]
    heads = [
        pltpu.make_async_copy(
            snap_hbm.at[w, q // 2 if q % 2 == 0 else nx - 1 - q // 2],
            first.at[z * slot_dev + w, q],
            load_sem.at[7 + w * AHEAD + q],
        )
        for w in range(slot_dev)
        for q in range(AHEAD)
    ]
    for head in heads:
        head.start()

    loads[0].start()

    for head in heads:
        head.wait()

    pl.semaphore_wait(barrier, 1 + sum(there.astype(jnp.int32) for there, _ in sides))

    y_from = pl.ds(pl.multiple_of(jnp.where(gy == 0, PAD + ny - 8, PAD), 8), 8)
    y_to = pl.ds(pl.multiple_of(jnp.where(gy == 0, PAD - 8, PAD + ny), 8), 8)

    def wide_halo(side):
        from_x, from_y, to_x, to_y = (
            (pl.ds(nx, W), body_y, pl.ds(0, W), body_y),
            (pl.ds(W, W), body_y, pl.ds(W + nx, W), body_y),
            (body_x, y_from, body_x, y_to),
        )[side]
        return pltpu.make_async_remote_copy(
            src_ref=field.at[0, from_x, from_y],
            dst_ref=field.at[0, to_x, to_y],
            send_sem=wide_send.at[side],
            recv_sem=wide_recv.at[side],
            device_id=across if side == 2 else sides[2 + side][1],
            device_id_type=MESH,
        )

    def x_halo(e, side, i):
        from_x = W + nx - 1 - i if side == 0 else W + i
        to_x = W - 1 - i if side == 0 else W + nx + i
        return pltpu.make_async_remote_copy(
            src_ref=field.at[e % 2, from_x, body_y],
            dst_ref=field.at[e % 2, to_x, body_y],
            send_sem=x_send.at[side, i],
            recv_sem=x_recv.at[e % 2, side, i],
            device_id=sides[2 + side][1],
            device_id_type=MESH,
        )

    def y_halo(e, q):
        x = W + spot(q)
        return pltpu.make_async_remote_copy(
            src_ref=field.at[e % 2, x, y_from],
            dst_ref=field.at[e % 2, x, y_to],
            send_sem=y_send.at[q],
            recv_sem=y_recv.at[e % 2, q],
            device_id=across,
            device_id_type=MESH,
        )

    def each_halo(e, q, act):
        for side in range(2):
            edge = (lax.rem(q, 2) == 1 - side) & (q < 2 * W)

            @pl.when(sides[2 + side][0] & edge)
            def _():
                act(x_halo(e, side, lax.div(q, 2)))

        act(y_halo(e, q))

    def halo_start(e, q):
        each_halo(e, q, lambda copy: copy.start())

    def halo_sent(e, q):
        each_halo(e, q, lambda copy: copy.wait_send())

    def halo_wait(e, q):
        for side in range(2):

            @pl.when(sides[2 + side][0] & (q == 0))
            def _():
                for i in range(W):
                    x_halo(e, 1 - side, i).wait_recv()

        y_halo(e, q).wait_recv()

    owner = [lax.div(slots[j], slot_dev) for j in range(n_snap)]

    def skipped(end):
        low = jnp.int32(n_snap)
        high = jnp.int32(-1)
        for j in range(n_snap):
            low = jnp.where(owner[j] == end, jnp.minimum(low, j), low)
            high = jnp.where(owner[j] == end, j, high)
        return (low, high)[:skips]

    not_up = skipped(n_probe - 1)
    not_down = skipped(0)

    up_way = (up, up_send, up_recv, {"probe": z + 1}, z < n_probe - 1)
    down_way = (down, down_send, down_recv, {"probe": z - 1}, z > 0)

    def link(way, ref, s):
        return pltpu.make_async_remote_copy(
            src_ref=ref,
            dst_ref=ref,
            send_sem=way[1].at[lax.rem(s + lag, ring)],
            recv_sem=way[2].at[lax.rem(s + lag, ring)],
            device_id=way[3],
            device_id_type=MESH,
        )

    def send(way, ref, s):
        @pl.when(way[4] & (s >= ring - lag))
        def _():
            link(way, ref, s).wait_send()

        @pl.when(way[4])
        def _():
            link(way, ref, s).start()

    def relay(s, way, hops, step, missing):
        buf = way[0]
        head = lag * hops

        @pl.when(s < head)
        def _():
            group = lax.div(s, lag)
            item = s - group * lag
            w = lax.div(item, AHEAD)
            ref = first.at[(z - step * (group + 1)) * slot_dev + w, item - w * AHEAD]
            link(way, ref, s - lag).wait_recv()
            send(way, ref, s)

        k = s - head

        @pl.when((k >= 0) & (k < total))
        def _():
            m = lax.div(k, run)
            x = spot(AHEAD + k - m * run)
            position = m
            for place in missing:
                position = position + jnp.where(position >= place, 1, 0)
            slot = slots[position]
            mine = lax.div(slot, slot_dev) == z
            which = lax.rem(slot, slot_dev)

            @pl.when(hops == 0)
            def _():
                buf[k] = own[which, x]

            @pl.when(hops > 0)
            def _():
                link(way, buf.at[k], s - lag).wait_recv()
                buf[k] = lax.select(mine, own[which, x], buf[k])

            send(way, buf.at[k], s)

    def comm(s):
        relay(s, up_way, z, 1, not_up)
        relay(s, down_way, n_probe - 1 - z, -1, not_down)

    def fetch(j, q):
        @pl.when(q < AHEAD)
        def _():
            frames[j % 3, q] = first[slots[j], q]

        @pl.when(q >= AHEAD)
        def _():
            def pick(buf, missing):
                count = sum(jnp.where(place < j, 1, 0) for place in missing)
                found = None
                for d in range(skips + 1):
                    if 0 <= j - d <= need[j]:
                        value = buf[(j - d) * run + q - AHEAD]
                        found = value if found is None else lax.select(count == d, value, found)
                return found

            from_up = owner[j] <= z
            for place in not_up:
                from_up = from_up & (place != j)
            frames[j % 3, q] = lax.select(from_up, pick(up, not_up), pick(down, not_down))

    weight = precond[ids[0]]

    def plane(n, q):
        a, b = n % 2, 1 - n % 2
        x = spot(q)
        if n > 0:
            halo_wait(n, q)
            halo_sent(n, q)
        if n == 0:
            fetch(0, q)
            fetch(1, q)
        fetch(n + 2, q)
        source = (
            frames[(n + 2) % 3, q].astype(jnp.float32)
            - 2.0 * frames[(n + 1) % 3, q].astype(jnp.float32)
            + frames[n % 3, q].astype(jnp.float32)
        )
        padded = field[a, x + W]
        high = padded.astype(jnp.bfloat16)
        low = (padded - high.astype(jnp.float32)).astype(jnp.bfloat16)
        lap = jnp.dot(
            ymat[...],
            jnp.concatenate([high, low, high], axis=0),
            preferred_element_type=jnp.float32,
        )
        high = high[PAD : PAD + ny]
        low = low[PAD : PAD + ny]
        lap = lap + jnp.dot(
            jnp.concatenate([high, low, high], axis=1),
            zmat[...],
            preferred_element_type=jnp.float32,
        )
        here = field[a, x + W, body_y]
        lap = lap + (3.0 * COEFFS[0]) * here
        for k in range(1, 5):
            lap = lap + COEFFS[k] * (field[a, x + W + k, body_y] + field[a, x + W - k, body_y])
        fresh = 2.0 * here - field[b, x + W, body_y] + cou[x] * lap - (weight * per[x]) * source
        if n == STEPS - 1:
            late[0, x] = fresh
            return
        field[b, x + W, body_y] = fresh
        halo_start(n + 1, q)
        if n == STEPS - 2:
            early[0, x] = fresh

    for item in range(lag):
        for way in (up_way, down_way):

            @pl.when(way[4])
            def _():
                ref = first.at[z * slot_dev + item // AHEAD, item % AHEAD]
                link(way, ref, item - lag).start()

    for load in loads[1:]:
        load.start()

    zero_plane = jnp.zeros((ny, nz), jnp.float32)
    zero_rows = jnp.zeros((8, nz), jnp.float32)
    shut = pl.ds(pl.multiple_of(jnp.where(gy == 0, PAD - 8, PAD + ny), 8), 8)
    for b in range(2):
        for end, x in ((n_gx - 1, W + nx), (0, 0)):

            @pl.when(gx == end)
            def _():
                for i in range(W):
                    field[b, x + i, body_y] = zero_plane

        def clear(x, b=b):
            for part in (pl.ds(0, PAD - 8), pl.ds(PAD + ny + 8, PAD - 8), shut):
                field[b, W + x, part] = zero_rows

        loop(0, nx, clear)

    loads[0].wait()
    lead = lag * (n_probe - 1)
    loop(0, lead, comm)
    loads[1].wait()
    for side in range(2):

        @pl.when(sides[2 + side][0])
        def _():
            wide_halo(side).start()

    wide_halo(2).start()

    loop(lead, lead + 2 * run, comm)
    for load in loads[2:]:
        load.wait()
    for side in range(2):

        @pl.when(sides[2 + side][0])
        def _():
            wide_halo(side).wait_send()
            wide_halo(1 - side).wait_recv()

    wide_halo(2).wait()

    lags = [0]
    for n in range(1, STEPS):
        lags.append(lags[-1] + 2 * W if need[n + 2] == need[n + 1] else 0)

    def done(n, g):
        ahead = g - nx * need[n + 2] - lags[n]
        if lags[n]:
            ahead = jnp.minimum(ahead, 2 * (ahead - W))
        return jnp.clip(ahead, 0, nx)

    def turn(g):
        m = lax.div(g, nx)
        q = g - m * nx

        @pl.when((q >= AHEAD) & (m < n_msg))
        def _():
            comm(lead + m * run + q - AHEAD)

        for n in range(STEPS):
            loop(done(n, g), done(n, g + 1), functools.partial(plane, n))

    loop(2 * nx, nx * n_msg + max(0, lags[-1]), turn)

    def finish(s):
        for way in (up_way, down_way):

            @pl.when(way[4])
            def _():
                link(way, way[0].at[0], s).wait_send()

    loop(0, ring, finish)


def store(early, late, early_hbm, late_hbm, sem):
    depth = early.shape[1] // PARTS
    copies = [
        pltpu.make_async_copy(
            src.at[0, pl.ds(i * depth, depth)], dst.at[0, pl.ds(i * depth, depth)], sem.at[j, i]
        )
        for i in range(PARTS)
        for j, (src, dst) in enumerate(((early, early_hbm), (late, late_hbm)))
    ]
    for copy in copies:
        copy.start()
    for copy in copies:
        copy.wait()


def steps(
    sizes, ident, skips, need, wave_prev, wave_cur, courant, perturb, snapshots, step_slots, precond, probe_ids
):
    nx, ny, nz = courant.shape
    slot_dev = snapshots.shape[0]
    total = (step_slots.shape[0] - skips) * (nx - AHEAD)
    ring = slot_dev * AHEAD * sizes[0]
    y_high, y_low = halves(band(ny, ny + 2 * PAD, PAD))
    z_high, z_low = halves(band(nz, nz, 0))
    ymat = jnp.asarray(np.concatenate([y_high, y_high, y_low], axis=1))
    zmat = jnp.asarray(np.concatenate([z_high, z_high, z_low], axis=0))
    smem = pl.BlockSpec(memory_space=pltpu.SMEM)
    vmem = pl.BlockSpec(memory_space=pltpu.VMEM)
    hbm = pl.BlockSpec(memory_space=pl.ANY)
    wave = pltpu.VMEM(wave_cur.shape, jnp.float32)
    dma = pltpu.SemaphoreType.DMA
    messages = pltpu.VMEM((total, ny, nz), jnp.bfloat16)
    results = pl.pallas_call(
        functools.partial(kernel, *sizes, skips, need),
        out_shape=(wave, wave),
        in_specs=[smem] * 3 + [hbm] * 7,
        out_specs=(vmem, vmem),
        scratch_shapes=[
            pltpu.VMEM(ymat.shape, jnp.bfloat16),
            pltpu.VMEM(zmat.shape, jnp.bfloat16),
            pltpu.VMEM((2, nx + 2 * W, ny + 2 * PAD, nz), jnp.float32),
            pltpu.VMEM((nx, ny, nz), jnp.float32),
            pltpu.VMEM((nx, ny, nz), jnp.float32),
            pltpu.VMEM((slot_dev, nx, ny, nz), jnp.bfloat16),
            pltpu.VMEM((sizes[0] * slot_dev, AHEAD, ny, nz), jnp.bfloat16),
            messages,
            messages,
            pltpu.VMEM((3, nx, ny, nz), jnp.bfloat16),
            dma((7 + slot_dev * AHEAD,)),
            dma((ring,)),
            dma((ring,)),
            dma((ring,)),
            dma((ring,)),
            dma((3,)),
            dma((3,)),
            dma((2, W)),
            dma((2, 2, W)),
            dma((nx,)),
            dma((2, nx)),
        ],
        compiler_params=pltpu.CompilerParams(
            collective_id=ident, has_side_effects=True, vmem_limit_bytes=54 * 1024 * 1024
        ),
    )(
        step_slots,
        precond,
        probe_ids,
        ymat,
        zmat,
        wave_prev,
        wave_cur,
        courant,
        perturb,
        snapshots,
    )
    return pl.pallas_call(
        store,
        out_shape=(jax.ShapeDtypeStruct(wave_cur.shape, jnp.float32),) * 2,
        in_specs=[vmem, vmem],
        out_specs=(hbm, hbm),
        scratch_shapes=[dma((2, PARTS))],
        compiler_params=pltpu.CompilerParams(vmem_limit_bytes=1024 * 1024),
    )(*results)


def choose(top, slots, pick):
    at = [slots[j] for j in range(slots.shape[0])]
    one = lambda flag: jnp.where(flag, 1, 0)
    side = [one(a < 2) + 2 * one(a > top - 2) for a in at]
    ends = sum(one(s > 0) for s in side)
    alone = sum(one(s == side[-1]) for s in side) == 1
    fixed = one((side[-1] > 0) & alone)
    four = 2 + one(side[-1] > 0) * (1 + one(side[-2] == side[-1]))
    pick[0] = jnp.where(ends == 4, four, fixed)


def shards(sizes, *args):
    snapshots, step_slots = args[4], args[5]
    n_probe, slot_dev = sizes[0], snapshots.shape[0]
    n_snap = step_slots.shape[0]

    def plan(skips):
        return tuple(min(j, n_snap - skips - 1) for j in range(n_snap))

    if slot_dev != 2 or n_snap != 6:
        return steps(sizes, 0, 1, plan(1), *args)
    smem = pl.BlockSpec(memory_space=pltpu.SMEM)
    pick = pl.pallas_call(
        functools.partial(choose, n_probe * slot_dev - 1),
        out_shape=pltpu.SMEM((1,), jnp.int32),
        in_specs=[smem],
        out_specs=smem,
    )(step_slots)
    plans = (
        (1, (0, 1, 2, 3, 3, 4)),
        (1, plan(1)),
        (2, (0, 1, 2, 2, 2, 3)),
        (2, (0, 1, 2, 2, 3, 3)),
        (2, plan(2)),
    )
    ways = [functools.partial(steps, sizes, i, *p) for i, p in enumerate(plans)]
    return lax.switch(pick[0], ways, *args)


def solution(mesh):
    placed = (
        P("probe", "gx", "gy", None),
        P("probe", "gx", "gy", None),
        P("gx", "gy", None),
        P("probe", "gx", "gy", None),
        P("probe", "gx", "gy", None),
        P(),
        P(),
        P("probe"),
    )
    sizes = (mesh.shape["probe"], mesh.shape["gx"], mesh.shape["gy"])
    return jax.shard_map(
        functools.partial(shards, sizes),
        mesh=mesh,
        in_specs=placed,
        out_specs=(P("probe", "gx", "gy", None), P("probe", "gx", "gy", None)),
        check_vma=False,
    )
```
